128 devices in a mesh: blk: 16 (over x_hi, y, core), bal: 8 (over x_lo, z).
Axes of the slice: x: 4 (x_hi: 2, x_lo: 2; x = x_hi * 2 + x_lo), y: 4, z: 4, core: 2. Of those that a mesh axis runs over, the one named last changes fastest.
Arguments:
- features: bfloat16 [131072, 512], P('blk', 'bal'), may hold values from -6 to 6
- tile_values: bfloat16 [16, 16, 32, 128, 128], P('blk'), may hold values from 0.049804688 to 1
- tile_rows: int32 [16, 16, 32], P('blk'), may hold values from 0 to 63
- tile_cols: int32 [16, 16, 32], P('blk'), may hold values from 0 to 63
- tile_counts: int32 [16, 16], P('blk'), may hold values from 8 to 32, as said below
- w_self: bfloat16 [512, 512], replicated, may hold values from -0.25 to 0.25
- w_neigh: bfloat16 [512, 512], replicated, may hold values from -6 to 6
- bias: float32 [512], replicated, may hold values from -3 to 3
- part_map: int32 [16, 64], P('blk'), may hold values from 0 to 7, as said below
Outputs:
- next_rows: bfloat16 [16, 8, 2048, 512], P('blk', 'bal')
The draws below stay inside these ranges and needn't reach their ends.
Inputs may be any that keep to these rules, and one draw needn't show every extreme that they name: `tile_counts`: live slots of one pair of vertex blocks; the most, 32, is reached by some pair in every draw. `part_map`: within one block of vertex rows at most 16 tiles go to any one value, and exactly 16 to some value.
All inputs are finite; a program needn't handle non-finite values.
Results may differ from the reference program's by a relative error of at most 0.0036.
Values may be sent and summed in bfloat16 or wider, within the bound.
No kernel may reach another device: no remote copies, remote signals or barrier semaphores. Data moves between devices by JAX's collectives and lax.ppermute only.
A program may use at most 128 MiB of HBM per device.

```python
import math
import jax
import jax.numpy as jnp
from jax import lax

F = 512
TILE = 128
S = 32
TR = 64
CAP = 16
R = 8192
N = 131072
N_BLK = 16
N_BAL = 8


def draw_tile_counts(key, part):
    counts = jax.random.randint(key, (N_BLK * N_BLK,), S // 4, S + 1)
    where_full = jax.random.randint(jax.random.fold_in(key, 1), (), 0, N_BLK * N_BLK)
    counts = counts.at[where_full].set(S)
    return counts.reshape(N_BLK, N_BLK).astype(jnp.int32)


def draw_part_map(key, part):

    def one_block(index):
        block_key = jax.random.fold_in(key, index)
        chosen = jax.random.randint(jax.random.fold_in(block_key, 1), (), 0, 2 * TR // CAP)
        perm = jax.random.permutation(jax.random.fold_in(block_key, 2), 2 * TR)
        seats = jnp.arange(2 * TR)
        scores = jnp.where(seats // CAP == chosen, perm - 2 * TR, perm)
        order = jnp.argsort(scores, stable=True)[:TR]
        return (order // CAP).astype(jnp.int32)
    return jax.vmap(one_block)(jnp.arange(N_BLK))


def touch_ends(result, own_key, least, largest):
    dims = result.shape
    index_at = [jax.random.randint(jax.random.fold_in(own_key, axis), (), 0, dims[axis]) for axis in range(len(dims))]
    result = result.at[tuple(index_at)].set(least)
    longest = dims.index(max(dims))
    index_at[longest] = (index_at[longest] + 1) % dims[longest]
    return result.at[tuple(index_at)].set(largest)


def block_scale(rng, extent, split, least, largest):
    level, own = 1.0, jax.random.fold_in(rng, 6)
    for dim, parts in split:
        heights = jnp.exp(jax.random.uniform(jax.random.fold_in(own, dim), (parts,), jnp.float32, least / len(split), largest / len(split)))
        level = level * jnp.repeat(heights, extent[dim] // parts).reshape([-1 if axis == dim else 1 for axis in range(len(extent))])
    return level


def gaussian(own_key, dims, scale, limit, split=(), kind=jnp.bfloat16):
    result = scale * jax.random.normal(own_key, dims, jnp.float32)
    if split:
        result = result * block_scale(own_key, dims, split, -0.22, 0.18)
    return jnp.clip(result, -limit, limit).astype(kind)


def setup_inputs(seed: int = 0) -> dict:
    keys = jax.random.split(jax.random.key(seed), 10)
    return {
        "features": gaussian(keys[0], (N, F), 1.0, 6.0, ((0, 16), (1, 8))),
        "tile_values": jnp.clip(jnp.exp(math.log(1.0) - 2.9996462 * jax.random.uniform(keys[1], (N_BLK, N_BLK, S, TILE, TILE), jnp.float32) ** block_scale(keys[1], (N_BLK, N_BLK, S, TILE, TILE), ((0, 16),), -0.2, 0.2)), 0.049804688, 1.0).astype(jnp.bfloat16),
        "tile_rows": touch_ends(jax.random.randint(keys[2], (N_BLK, N_BLK, S), 0, TR), jax.random.fold_in(keys[2], 1), 0, TR - 1).astype(jnp.int32),
        "tile_cols": touch_ends(jax.random.randint(keys[3], (N_BLK, N_BLK, S), 0, TR), jax.random.fold_in(keys[3], 1), 0, TR - 1).astype(jnp.int32),
        "tile_counts": draw_tile_counts(jax.random.fold_in(keys[9], 71), 0),
        "w_self": gaussian(keys[5], (F, F), F ** -0.5, 0.25),
        "w_neigh": gaussian(keys[6], (F, F), (0.5 * (N_BLK * S * TILE // TR) ** 0.5 / F ** 0.5), 6.0),
        "bias": gaussian(keys[7], (F,), 0.5, 3.0, (), jnp.float32),
        "part_map": draw_part_map(jax.random.fold_in(keys[9], 71), 0),
    }


def arrange_rows(hidden_block, pm):
    dest_hot = (pm[:, None] == jnp.arange(N_BAL)[None, :]).astype(jnp.int32)
    ranks = jnp.cumsum(dest_hot, axis=0) - dest_hot
    place = pm * CAP + jnp.sum(ranks * dest_hot, axis=1)
    select = (jnp.arange(N_BAL * CAP)[:, None] == place[None, :]).astype(jnp.float32)
    tiles = hidden_block.reshape(TR, TILE, F).astype(jnp.float32)
    placed = jnp.einsum('kt,tif->kif', select, tiles, precision=lax.Precision.HIGHEST)
    return placed.astype(jnp.bfloat16).reshape(N_BAL, CAP * TILE, F)


def reference(features, tile_values, tile_rows, tile_cols, tile_counts, w_self, w_neigh, bias, part_map):
    feats = features.reshape(N_BLK, TR, TILE, F)

    def one_block(inputs):
        values, rows_idx, cols_idx, counts = inputs
        live = jnp.arange(S)[None, :] < counts[:, None]
        row_hot = ((rows_idx[:, :, None] == jnp.arange(TR)[None, None, :]) & live[:, :, None]).astype(jnp.float32)

        def per_source(total, piece):
            vals, picks, hot, source = piece
            gathered = jnp.take(feats[source], picks, axis=0)
            prod = jnp.einsum('sij,sjf->sif', vals.astype(jnp.float32), gathered.astype(jnp.float32), precision=lax.Precision.HIGHEST)
            return total + jnp.einsum('st,sif->tif', hot, prod, precision=lax.Precision.HIGHEST), None

        start = jnp.zeros((TR, TILE, F), jnp.float32)
        total, unused = lax.scan(per_source, start, (values, cols_idx, row_hot, jnp.arange(N_BLK)))
        mass = jnp.sum(values.astype(jnp.float32), axis=-1)
        degree = 1.0 + jnp.einsum('cst,csi->ti', row_hot, mass, precision=lax.Precision.HIGHEST)
        return (total / degree[:, :, None]).astype(jnp.bfloat16).reshape(TR * TILE, F)

    mean_agg = lax.map(one_block, (tile_values, tile_rows, tile_cols, tile_counts)).reshape(N, F)
    pre = jnp.dot(features, w_self, preferred_element_type=jnp.float32)
    pre = pre + jnp.dot(mean_agg, w_neigh, preferred_element_type=jnp.float32) + bias
    hidden = jnp.maximum(pre, 0.0).astype(jnp.bfloat16).reshape(N_BLK, R, F)
    return jax.vmap(arrange_rows)(hidden, part_map)
```

```python
import functools

import jax
import jax.numpy as jnp
from jax import lax
from jax.experimental import pallas as pl
from jax.experimental.pallas import tpu as pltpu
from jax.sharding import PartitionSpec as P

TILE = 128
CHUNKS = 1
ONES = 16
UNROLL = 8


def spot(position):
    return position // 8, (position // 2) % 4, position % 2


def route(block, dx, dy, dc):
    pairs = []
    for source in range(16):
        x, y, c = spot(source)
        pairs.append((source, ((x + dx) % 2) * 8 + ((y + dy) % 4) * 2 + (c + dc) % 2))
    return lax.ppermute(block, "blk", pairs)


def absorb(acc_ref, halves, source, counts, rows, cols, v_ref, with_ones):
    live = counts[source]
    dummy = acc_ref.shape[0] - 1

    def step(group, carry):
        found = []
        for u in range(UNROLL):
            slot = group * UNROLL + u
            start = pl.multiple_of(cols[source, slot] * TILE, TILE)
            parts = [ref[:, pl.ds(start, TILE)] for ref in halves]
            if with_ones:
                parts.append(jnp.ones((ONES, TILE), jnp.bfloat16))
            left = parts[0] if len(parts) == 1 else jnp.concatenate(parts, axis=0)
            prod = lax.dot_general(
                left, v_ref[slot], (((1,), (1,)), ((), ())), preferred_element_type=jnp.float32
            )
            found.append((jnp.where(slot < live, rows[source, slot], dummy), prod))
        for target, prod in found:
            acc_ref[target] += prod
        return carry

    lax.fori_loop(0, (live + UNROLL - 1) // UNROLL, step, 0)


def seat(here, dx, dy, dc):
    x, y, c = here // 8, (here // 2) % 4, here % 2
    return ((x + dx) % 2) * 8 + ((y + dy) % 4) * 2 + (c + dc) % 2


def gather_kernel(layout, offsets, first, with_ones, here, counts, rows, cols, v_hbm, *refs):
    n_blocks = sum(layout)
    n = len(layout)
    blocks = refs[:n_blocks]
    acc_ref, v_ref, v_sem, b_sem = refs[n_blocks + (0 if first else 1) :][:4]
    staged = refs[-n_blocks:]
    places = [seat(here[0], *offsets[i]) for i in range(n)]
    copies = []
    at = 0
    for i, width in enumerate(layout):
        mine = [pltpu.make_async_copy(v_hbm.at[places[i]], v_ref.at[i], v_sem.at[i])]
        for j in range(at, at + width):
            mine.append(pltpu.make_async_copy(blocks[j], staged[j], b_sem.at[j]))
        at += width
        copies.append(mine)
        for copy in mine:
            copy.start()
    if first:
        acc_ref[...] = jnp.zeros_like(acc_ref)
    else:
        acc_ref[...] = refs[n_blocks][...]
    at = 0
    for i, width in enumerate(layout):
        for copy in copies[i]:
            copy.wait()
        absorb(
            acc_ref, staged[at : at + width], places[i], counts, rows, cols, v_ref.at[i], with_ones
        )
        at += width


def accumulate(acc, groups, offsets, here, tables, values, height, tiles_per, with_ones):
    counts, rows, cols = tables
    layout = tuple(len(g) for g in groups)
    blocks = [b for g in groups for b in g]
    first = acc is None
    vmem = pl.BlockSpec(memory_space=pltpu.VMEM)
    smem = pl.BlockSpec(memory_space=pltpu.SMEM)
    anywhere = pl.BlockSpec(memory_space=pl.ANY)
    operands = [here.reshape(1), counts, rows, cols, values] + blocks
    specs = [smem] * 4 + [anywhere] * (1 + len(blocks))
    if not first:
        operands.append(acc)
        specs.append(vmem)
    return pl.pallas_call(
        functools.partial(gather_kernel, layout, tuple(offsets), first, with_ones),
        in_specs=specs,
        out_specs=vmem,
        out_shape=jax.ShapeDtypeStruct(
            (tiles_per + 1, height + (ONES if with_ones else 0), TILE), jnp.float32
        ),
        scratch_shapes=[
            pltpu.VMEM((len(groups),) + values.shape[1:], values.dtype),
            pltpu.SemaphoreType.DMA((len(groups),)),
            pltpu.SemaphoreType.DMA((len(blocks),)),
        ]
        + [pltpu.VMEM(b.shape, b.dtype) for b in blocks],
        name="aggregate",
    )(*operands)


def place_into(out_ref, mapping, used, tiles_per, tile_of):
    n_bal = out_ref.shape[0]
    out_ref[...] = jnp.zeros_like(out_ref)
    for d in range(n_bal):
        used[d] = 0

    def step(t, carry):
        d = mapping[0, t]
        k = used[d]
        used[d] = k + 1
        out_ref[d, :, pl.ds(pl.multiple_of(k * TILE, TILE), TILE)] = tile_of(t)
        return carry

    lax.fori_loop(0, tiles_per, step, 0)


def place_kernel(mapping, x_ref, out_ref, used):
    tiles_per = mapping.shape[1]
    place_into(
        out_ref, mapping, used, tiles_per,
        lambda t: x_ref[:, pl.ds(pl.multiple_of(t * TILE, TILE), TILE)],
    )


def place_features(block, mapping, n_bal, capacity):
    return pl.pallas_call(
        place_kernel,
        in_specs=[pl.BlockSpec(memory_space=pltpu.SMEM), pl.BlockSpec(memory_space=pltpu.VMEM)],
        out_specs=pl.BlockSpec(memory_space=pltpu.VMEM),
        out_shape=jax.ShapeDtypeStruct((n_bal, block.shape[0], capacity * TILE), block.dtype),
        scratch_shapes=[pltpu.SMEM((n_bal,), jnp.int32)],
        name="place_features",
    )(mapping, block)


def mean_kernel(height, mapping, acc_ref, deg_ref, out_ref, used):
    tiles_per = mapping.shape[1]

    def tile_of(t):
        inverse = 1.0 / (1.0 + deg_ref[t, 0:1, :])
        return (acc_ref[t, 0:height, :] * inverse).astype(jnp.bfloat16)

    place_into(out_ref, mapping, used, tiles_per, tile_of)


def place_means(acc, degree, height, mapping, n_bal, capacity):
    vmem = pl.BlockSpec(memory_space=pltpu.VMEM)
    return pl.pallas_call(
        functools.partial(mean_kernel, height),
        in_specs=[pl.BlockSpec(memory_space=pltpu.SMEM), vmem, vmem],
        out_specs=vmem,
        out_shape=jax.ShapeDtypeStruct((n_bal, height, capacity * TILE), jnp.bfloat16),
        scratch_shapes=[pltpu.SMEM((n_bal,), jnp.int32)],
        name="place_means",
    )(mapping, acc, degree)


def exchange(placed):
    got = lax.all_to_all(placed, "bal", split_axis=0, concat_axis=0, tiled=True)
    return got.reshape(got.shape[0] * got.shape[1], got.shape[2])


def across(left, right):
    return lax.dot_general(
        left, right, (((0,), (0,)), ((), ())), preferred_element_type=jnp.float32
    )


def on_device(
    features, tile_values, tile_rows, tile_cols, tile_counts, w_self, w_neigh, bias, part_map
):
    n_bal = lax.axis_size("bal")
    here = lax.axis_index("blk")
    column = lax.axis_index("bal")
    tiles_per = part_map.shape[1]
    capacity = 2 * tiles_per // n_bal
    width = features.shape[1]
    height = width // CHUNKS
    values = tile_values[0]
    tables = (tile_counts[0], tile_rows[0], tile_cols[0])
    flipped = features.T

    mine = exchange(place_features(flipped, part_map, n_bal, capacity))
    pre = across(mine, w_self)
    degree = None
    w_chunks = w_neigh.reshape(n_bal, CHUNKS, height, w_neigh.shape[1])
    for k in range(CHUNKS):
        own = flipped[k * height : (k + 1) * height]
        half = height // 2
        near = [own, route(own, 1, 0, 0)]
        stages = [[], [], []]
        for dx, block in enumerate(near):
            up = route(block, 0, 1, 0)
            down = route(block, 0, -1, 0)
            top = route(up[:half], 0, 1, 0)
            bottom = route(down[half:], 0, -1, 0)
            stages[0].append(((block,), (dx, 0)))
            stages[1].append(((up,), (dx, -1)))
            stages[1].append(((down,), (dx, 1)))
            stages[2].append(((top, bottom), (dx, 2)))
        acc = None
        with_ones = k == 0
        for stage in stages:
            groups, offsets = [], []
            for dc in range(2):
                for blocks, (dx, dy) in stage:
                    groups.append([b if dc == 0 else route(b, 0, 0, 1) for b in blocks])
                    offsets.append((dx, dy, dc))
            acc = accumulate(
                acc, groups, offsets, here, tables, values, height, tiles_per, with_ones
            )
        if degree is None:
            degree = acc[:, height : height + 8, :]
        means = exchange(place_means(acc, degree, height, part_map, n_bal, capacity))
        weight = w_chunks[:, k].reshape(n_bal * height, w_neigh.shape[1])
        pre = pre + across(means, weight)
    filled = jnp.sum((part_map[0] == column).astype(jnp.int32)) * TILE
    row = lax.broadcasted_iota(jnp.int32, (capacity * TILE, 1), 0)
    hidden = jnp.where(row < filled, jnp.maximum(pre + bias[None, :], 0.0), 0.0)
    return hidden.astype(jnp.bfloat16)[None, None]


def solution(mesh):
    placed = (
        P("blk", "bal"),
        P("blk", None, None, None, None),
        P("blk", None, None),
        P("blk", None, None),
        P("blk", None),
        P(),
        P(),
        P(),
        P("blk", None),
    )
    return jax.shard_map(
        on_device,
        mesh=mesh,
        in_specs=placed,
        out_specs=P("blk", "bal", None, None),
        check_vma=False,
    )
```

```python
import functools

import jax
import jax.numpy as jnp
from jax import lax
from jax.experimental import pallas as pl
from jax.experimental.pallas import tpu as pltpu
from jax.sharding import PartitionSpec as P

TILE = 128
ONES = 16
UNROLL = 8


def spot(position):
    return position // 8, (position // 2) % 4, position % 2


def route(block, dx, dy, dc):
    pairs = []
    for source in range(16):
        x, y, c = spot(source)
        pairs.append((source, ((x + dx) % 2) * 8 + ((y + dy) % 4) * 2 + (c + dc) % 2))
    return lax.ppermute(block, "blk", pairs)


def absorb(acc_ref, halves, source, counts, rows, cols, v_ref, with_ones):
    live = counts[source]
    dummy = acc_ref.shape[0] - 1

    def step(group, carry):
        found = []
        for u in range(UNROLL):
            slot = group * UNROLL + u
            start = pl.multiple_of(cols[source, slot] * TILE, TILE)
            parts = [ref[:, pl.ds(start, TILE)] for ref in halves]
            if with_ones:
                parts.append(jnp.ones((ONES, TILE), jnp.bfloat16))
            left = parts[0] if len(parts) == 1 else jnp.concatenate(parts, axis=0)
            prod = lax.dot_general(
                left, v_ref[slot], (((1,), (1,)), ((), ())), preferred_element_type=jnp.float32
            )
            found.append((jnp.where(slot < live, rows[source, slot], dummy), prod))
        for target, prod in found:
            acc_ref[target] += prod
        return carry

    lax.fori_loop(0, (live + UNROLL - 1) // UNROLL, step, 0)


def seat(here, dx, dy, dc):
    x, y, c = here // 8, (here // 2) % 4, here % 2
    return ((x + dx) % 2) * 8 + ((y + dy) % 4) * 2 + (c + dc) % 2


def gather_kernel(layout, offsets, height, first, last, here, counts, rows, cols, *refs):
    refs = list(refs)
    mapping = refs.pop(0) if last else None
    v_hbm = refs.pop(0)
    n_blocks = sum(layout)
    n = len(layout)
    blocks = [refs.pop(0) for i in range(n_blocks)]
    acc_in = None if first else refs.pop(0)
    out_ref = refs.pop(0)
    v_ref, v_sem, b_sem = refs.pop(0), refs.pop(0), refs.pop(0)
    staged = [refs.pop(0) for i in range(n_blocks)]
    if last:
        acc_ref, a_sem, used = refs
    else:
        acc_ref = out_ref
        (a_sem,) = refs
    places = [seat(here[0], *offsets[i]) for i in range(n)]
    loads = []
    if not first:
        if last:
            at = (last - 1) * height
            pieces = [(at, 0, height), (acc_in.shape[1] - ONES, height, ONES)]
        else:
            pieces = [(0, 0, acc_in.shape[1])]
        for k, (src, dst, size) in enumerate(pieces):
            loads.append(
                pltpu.make_async_copy(
                    acc_in.at[:, pl.ds(src, size), :], acc_ref.at[:, pl.ds(dst, size), :], a_sem.at[k]
                )
            )
    for copy in loads:
        copy.start()
    copies = []
    at = 0
    for i, width in enumerate(layout):
        mine = [pltpu.make_async_copy(v_hbm.at[places[i]], v_ref.at[i], v_sem.at[i])]
        for j in range(at, at + width):
            mine.append(pltpu.make_async_copy(blocks[j], staged[j], b_sem.at[j]))
        at += width
        copies.append(mine)
        for copy in mine:
            copy.start()
    if first:
        acc_ref[...] = jnp.zeros_like(acc_ref)
    if last:
        out_ref[...] = jnp.zeros_like(out_ref)
    for copy in loads:
        copy.wait()
    at = 0
    for i, width in enumerate(layout):
        for copy in copies[i]:
            copy.wait()
        absorb(acc_ref, staged[at : at + width], places[i], counts, rows, cols, v_ref.at[i], True)
        at += width
    if last:

        def tile_of(t):
            inverse = 1.0 / (1.0 + acc_ref[t, height : height + 1, :])
            return (acc_ref[t, 0:height, :] * inverse).astype(jnp.bfloat16)

        place_into(out_ref, mapping, used, mapping.shape[1], tile_of)


def accumulate(acc, groups, offsets, here, tables, values, tiles_per, last=0, mapping=None, out=None):
    counts, rows, cols = tables
    layout = tuple(len(g) for g in groups)
    blocks = [b for g in groups for b in g]
    height = sum(b.shape[0] for b in groups[0])
    first = acc is None
    vmem = pl.BlockSpec(memory_space=pltpu.VMEM)
    smem = pl.BlockSpec(memory_space=pltpu.SMEM)
    anywhere = pl.BlockSpec(memory_space=pl.ANY)
    operands = [here.reshape(1), counts, rows, cols]
    if last:
        operands.append(mapping)
    specs = [smem] * len(operands) + [anywhere] * (1 + len(blocks))
    operands += [values] + blocks
    if not first:
        operands.append(acc)
        specs.append(anywhere)
    shape = (tiles_per + 1, height + ONES, TILE)
    scratch = [
        pltpu.VMEM((len(groups),) + values.shape[1:], values.dtype),
        pltpu.SemaphoreType.DMA((len(groups),)),
        pltpu.SemaphoreType.DMA((len(blocks),)),
    ] + [pltpu.VMEM(b.shape, b.dtype) for b in blocks]
    if last:
        scratch.append(pltpu.VMEM(shape, jnp.float32))
    scratch.append(pltpu.SemaphoreType.DMA((2,)))
    if last:
        scratch.append(pltpu.SMEM((out[0],), jnp.int32))
        result = jax.ShapeDtypeStruct((out[0], height, out[1]), jnp.bfloat16)
    else:
        result = jax.ShapeDtypeStruct(shape, jnp.float32)
    return pl.pallas_call(
        functools.partial(gather_kernel, layout, tuple(offsets), height, first, last),
        in_specs=specs,
        out_specs=vmem,
        out_shape=result,
        scratch_shapes=scratch,
        name="aggregate_last" if last else "aggregate",
    )(*operands)


def place_into(out_ref, mapping, used, tiles_per, tile_of):
    n_bal = out_ref.shape[0]
    out_ref[...] = jnp.zeros_like(out_ref)
    for d in range(n_bal):
        used[d] = 0

    def step(t, carry):
        d = mapping[0, t]
        k = used[d]
        used[d] = k + 1
        out_ref[d, :, pl.ds(pl.multiple_of(k * TILE, TILE), TILE)] = tile_of(t)
        return carry

    lax.fori_loop(0, tiles_per, step, 0)


def place_kernel(mapping, x_ref, out_ref, used):
    tiles_per = mapping.shape[1]
    place_into(
        out_ref, mapping, used, tiles_per,
        lambda t: x_ref[:, pl.ds(pl.multiple_of(t * TILE, TILE), TILE)],
    )


def place_features(block, mapping, n_bal, capacity):
    return pl.pallas_call(
        place_kernel,
        in_specs=[pl.BlockSpec(memory_space=pltpu.SMEM), pl.BlockSpec(memory_space=pltpu.VMEM)],
        out_specs=pl.BlockSpec(memory_space=pltpu.VMEM),
        out_shape=jax.ShapeDtypeStruct((n_bal, block.shape[0], capacity * TILE), block.dtype),
        scratch_shapes=[pltpu.SMEM((n_bal,), jnp.int32)],
        name="place_features",
    )(mapping, block)


def exchange(placed):
    got = lax.all_to_all(placed, "bal", split_axis=0, concat_axis=0, tiled=True)
    return got.reshape(got.shape[0] * got.shape[1], got.shape[2])


def across(left, right):
    return lax.dot_general(
        left, right, (((0,), (0,)), ((), ())), preferred_element_type=jnp.float32
    )


def on_device(
    features, tile_values, tile_rows, tile_cols, tile_counts, w_self, w_neigh, bias, part_map
):
    n_bal = lax.axis_size("bal")
    here = lax.axis_index("blk")
    column = lax.axis_index("bal")
    tiles_per = part_map.shape[1]
    capacity = 2 * tiles_per // n_bal
    width = features.shape[1]
    half = width // 2
    values = tile_values[0]
    tables = (tile_counts[0], tile_rows[0], tile_cols[0])
    own = features.T
    placing = (n_bal, capacity * TILE)

    def gathered(acc, pieces, **extra):
        groups, offsets = [], []
        for dc in range(2):
            for blocks, twins, (dx, dy) in pieces:
                groups.append(list(blocks if dc == 0 else twins))
                offsets.append((dx, dy, dc))
        return accumulate(acc, groups, offsets, here, tables, values, tiles_per, **extra)

    def twin(*blocks):
        return [route(b, 0, 0, 1) for b in blocks]

    side = route(own, 1, 0, 0)
    up = route(own, 0, 1, 0)
    down = route(own, 0, -1, 0)
    own_twin = twin(own)
    mine = exchange(place_features(own, part_map, n_bal, capacity))
    acc = gathered(None, [([own], own_twin, (0, 0))])
    side, up, down, acc = lax.optimization_barrier((side, up, down, acc))
    top = route(up[:half], 0, 1, 0)
    bottom = route(down[half:], 0, -1, 0)
    parts = [side[:half], side[half:]]
    ups = [route(p, 0, 1, 0) for p in parts]
    downs = [route(p, 0, -1, 0) for p in parts]
    acc = gathered(
        acc,
        [
            ([side], twin(side), (1, 0)),
            ([up], twin(up), (0, -1)),
            ([down], twin(down), (0, 1)),
        ],
    )
    top, bottom, acc = lax.optimization_barrier((top, bottom, acc))
    far = [route(top, 1, 0, 0), route(bottom, 1, 0, 0)]
    acc = gathered(acc, [([top, bottom], twin(top, bottom), (0, 2))])
    far[0], ups[1], downs[1], acc = lax.optimization_barrier((far[0], ups[1], downs[1], acc))
    w_parts = w_neigh.reshape(n_bal, 2, half, w_neigh.shape[1])
    pre = across(mine, w_self)
    for k in range(2):
        placed = gathered(
            acc,
            [
                ([ups[k]], twin(ups[k]), (1, -1)),
                ([downs[k]], twin(downs[k]), (1, 1)),
                ([far[k]], twin(far[k]), (1, 2)),
            ],
            last=k + 1,
            mapping=part_map,
            out=placing,
        )
        means = exchange(placed)
        weight = w_parts[:, k].reshape(n_bal * half, w_neigh.shape[1])
        pre = pre + across(means, weight)
    filled = jnp.sum((part_map[0] == column).astype(jnp.int32)) * TILE
    row = lax.broadcasted_iota(jnp.int32, (capacity * TILE, 1), 0)
    hidden = jnp.where(row < filled, jnp.maximum(pre + bias[None, :], 0.0), 0.0)
    return hidden.astype(jnp.bfloat16)[None, None]


def solution(mesh):
    placed = (
        P("blk", "bal"),
        P("blk", None, None, None, None),
        P("blk", None, None),
        P("blk", None, None),
        P("blk", None),
        P(),
        P(),
        P(),
        P("blk", None),
    )
    return jax.shard_map(
        on_device,
        mesh=mesh,
        in_specs=placed,
        out_specs=P("blk", "bal", None, None),
        check_vma=False,
    )
```

```python
import functools

import jax
import jax.numpy as jnp
from jax import lax
from jax.experimental import pallas as pl
from jax.experimental.pallas import tpu as pltpu
from jax.sharding import PartitionSpec as P

TILE = 128
ONES = 16
UNROLL = 8
AHEAD = 3
SPLIT = 8


def spot(position):
    return position // 8, (position // 2) % 4, position % 2


def route(block, dx, dy, dc):
    pairs = []
    for source in range(16):
        x, y, c = spot(source)
        pairs.append((source, ((x + dx) % 2) * 8 + ((y + dy) % 4) * 2 + (c + dc) % 2))
    return lax.ppermute(block, "blk", pairs)


def absorb(acc_ref, halves, source, table, v_ref):
    slots = v_ref.shape[0]
    live = table[source, 2 * slots]
    dummy = acc_ref.shape[0] - 1

    def step(group, carry):
        found = []
        for u in range(UNROLL):
            slot = group * UNROLL + u
            start = pl.multiple_of(table[source, slots + slot] * TILE, TILE)
            parts = [ref[:, pl.ds(start, TILE)] for ref in halves]
            parts.append(jnp.ones((ONES, TILE), jnp.bfloat16))
            left = jnp.concatenate(parts, axis=0)
            prod = lax.dot_general(
                left, v_ref[slot], (((1,), (1,)), ((), ())), preferred_element_type=jnp.float32
            )
            found.append((jnp.where(slot < live, table[source, slot], dummy), prod))
        for target, prod in found:
            acc_ref[target] += prod
        return carry

    lax.fori_loop(0, (live + UNROLL - 1) // UNROLL, step, 0)


def seat(here, dx, dy, dc):
    x, y, c = here // 8, (here // 2) % 4, here % 2
    return ((x + dx) % 2) * 8 + ((y + dy) % 4) * 2 + (c + dc) % 2


def begin(copy):
    copy.start()


def finish(copy):
    copy.wait()


def act_on(act, make, i, q):
    act(make(i, q))


def gather_kernel(layout, offsets, height, first, last, table, *refs):
    refs = list(refs)
    v_hbm = refs.pop(0)
    n_blocks = sum(layout)
    n = len(layout)
    blocks = [refs.pop(0) for i in range(n_blocks)]
    acc_in = None if first else refs.pop(0)
    out_ref = refs.pop(0)
    v_ref, v_sem, b_sem = refs.pop(0), refs.pop(0), refs.pop(0)
    staged = [refs.pop(0) for i in range(n_blocks)]
    acc_ref, a_sem, o_sem = refs.pop(0), refs.pop(0), refs.pop(0)
    made_ref, used = refs if last else (acc_ref, None)
    slots = v_ref.shape[1]
    here = table[0, 2 * slots + 1]
    places = [seat(here, *offsets[i]) for i in range(n)]
    tiles_per = acc_ref.shape[0] - 1
    span = tiles_per // SPLIT
    loads = []
    if not first:
        for k in range(SPLIT):
            part = pl.ds(k * span, span)
            loads.append(pltpu.make_async_copy(acc_in.at[part], acc_ref.at[part], a_sem.at[k]))
    for copy in loads:
        copy.start()
    parts = v_ref.shape[1] // UNROLL
    begins = [sum(layout[:i]) for i in range(n)]

    def values_copy(i, q):
        part = pl.ds(q * UNROLL, UNROLL)
        return pltpu.make_async_copy(
            v_hbm.at[places[i], part], v_ref.at[i, part], v_sem.at[i * parts + q]
        )

    def each(i, act):
        for j in range(begins[i], begins[i] + layout[i]):
            act(pltpu.make_async_copy(blocks[j], staged[j], b_sem.at[j]))
        for q in range(parts):
            pl.when(table[places[i], 2 * slots] > q * UNROLL)(functools.partial(act_on, act, values_copy, i, q))

    for i in range(min(AHEAD, n)):
        each(i, begin)
    if first:
        acc_ref[...] = jnp.zeros_like(acc_ref)
    if last:
        made_ref[...] = jnp.zeros_like(made_ref)
    for copy in loads:
        copy.wait()
    for i, width in enumerate(layout):
        if i + AHEAD < n:
            each(i + AHEAD, begin)
        each(i, finish)
        absorb(
            acc_ref, staged[begins[i] : begins[i] + width], places[i], table, v_ref.at[i]
        )
    if last:

        def tile_of(t):
            inverse = 1.0 / (1.0 + acc_ref[t, height : height + 1, :])
            return (acc_ref[t, 0:height, :] * inverse).astype(jnp.bfloat16)

        place_into(made_ref, table, used, tiles_per, tile_of)
    step = out_ref.shape[0] // SPLIT
    stores = [
        pltpu.make_async_copy(
            made_ref.at[pl.ds(k * step, step)], out_ref.at[pl.ds(k * step, step)], o_sem.at[k]
        )
        for k in range(SPLIT)
    ]
    for copy in stores:
        copy.start()
    for copy in stores:
        copy.wait()


def accumulate(acc, groups, offsets, table, values, tiles_per, last=False, out=None):
    layout = tuple(len(g) for g in groups)
    blocks = [b for g in groups for b in g]
    height = sum(b.shape[0] for b in groups[0])
    first = acc is None
    smem = pl.BlockSpec(memory_space=pltpu.SMEM)
    anywhere = pl.BlockSpec(memory_space=pl.ANY)
    operands = [table]
    specs = [smem] + [anywhere] * (1 + len(blocks))
    operands += [values] + blocks
    if not first:
        operands.append(acc)
        specs.append(anywhere)
    shape = (tiles_per, height + ONES, TILE)
    scratch = [
        pltpu.VMEM((len(groups),) + values.shape[1:], values.dtype),
        pltpu.SemaphoreType.DMA((len(groups) * (values.shape[1] // UNROLL),)),
        pltpu.SemaphoreType.DMA((len(blocks),)),
    ] + [pltpu.VMEM(b.shape, b.dtype) for b in blocks]
    scratch += [
        pltpu.VMEM((tiles_per + 1,) + shape[1:], jnp.float32),
        pltpu.SemaphoreType.DMA((SPLIT,)),
        pltpu.SemaphoreType.DMA((SPLIT,)),
    ]
    if last:
        made = (out[0], height, out[1])
        scratch += [pltpu.VMEM(made, jnp.bfloat16), pltpu.SMEM((out[0],), jnp.int32)]
        result = jax.ShapeDtypeStruct(made, jnp.bfloat16)
    else:
        result = jax.ShapeDtypeStruct(shape, jnp.float32)
    return pl.pallas_call(
        functools.partial(gather_kernel, layout, tuple(offsets), height, first, last),
        in_specs=specs,
        out_specs=anywhere,
        out_shape=result,
        scratch_shapes=scratch,
        cost_estimate=pl.CostEstimate(
            flops=0, transcendentals=0, bytes_accessed=(8 + 3 * len(groups)) * 2**20
        ),
        name="aggregate_last" if last else "aggregate",
    )(*operands)


def place_into(out_ref, mapping, used, tiles_per, tile_of):
    n_bal = out_ref.shape[0]
    out_ref[...] = jnp.zeros_like(out_ref)
    for d in range(n_bal):
        used[d] = 0

    def step(t, carry):
        d = mapping[mapping.shape[0] - 1, t]
        k = used[d]
        used[d] = k + 1
        out_ref[d, :, pl.ds(pl.multiple_of(k * TILE, TILE), TILE)] = tile_of(t)
        return carry

    lax.fori_loop(0, tiles_per, step, 0, unroll=8)


def place_kernel(mapping, x_ref, out_ref, used):
    tiles_per = x_ref.shape[1] // TILE
    place_into(
        out_ref, mapping, used, tiles_per,
        lambda t: x_ref[:, pl.ds(pl.multiple_of(t * TILE, TILE), TILE)],
    )


def place_features(block, mapping, n_bal, capacity):
    return pl.pallas_call(
        place_kernel,
        in_specs=[pl.BlockSpec(memory_space=pltpu.SMEM), pl.BlockSpec(memory_space=pltpu.VMEM)],
        out_specs=pl.BlockSpec(memory_space=pltpu.VMEM),
        out_shape=jax.ShapeDtypeStruct((n_bal, block.shape[0], capacity * TILE), block.dtype),
        scratch_shapes=[pltpu.SMEM((n_bal,), jnp.int32)],
        cost_estimate=pl.CostEstimate(flops=0, transcendentals=0, bytes_accessed=8 * 2**20),
        name="place_features",
    )(mapping, block)


def fit(table):
    return jnp.pad(table, ((0, 0), (0, TILE - table.shape[1])))


def exchange(placed):
    got = lax.all_to_all(placed, "bal", split_axis=0, concat_axis=0, tiled=True)
    return got.reshape(got.shape[0] * got.shape[1], got.shape[2])


def across(left, right):
    return lax.dot_general(
        left, right, (((0,), (0,)), ((), ())), preferred_element_type=jnp.float32
    )


def on_device(
    features, tile_values, tile_rows, tile_cols, tile_counts, w_self, w_neigh, bias, part_map
):
    n_blk = lax.axis_size("blk")
    n_bal = lax.axis_size("bal")
    here = lax.axis_index("blk")
    column = lax.axis_index("bal")
    tiles_per = part_map.shape[1]
    capacity = 2 * tiles_per // n_bal
    width = features.shape[1]
    half = width // 2
    values = tile_values[0]
    table = jnp.concatenate(
        [tile_rows[0], tile_cols[0], tile_counts[0][:, None], jnp.full((n_blk, 1), here)], axis=1
    ).astype(jnp.int32)
    table = jnp.concatenate([fit(table), fit(part_map.astype(jnp.int32))], axis=0)
    own = features.T
    placing = (n_bal, capacity * TILE)

    def gathered(acc, pieces, **extra):
        groups = [list(blocks) for blocks, offset in pieces]
        offsets = [offset for blocks, offset in pieces]
        return accumulate(acc, groups, offsets, table, values, tiles_per, **extra)

    def twin(block):
        return route(block, 0, 0, 1)

    side = route(own, 1, 0, 0)
    up = route(own, 0, 1, 0)
    down = route(own, 0, -1, 0)
    mine = place_features(own, table, n_bal, capacity)
    acc = gathered(None, [([own], (0, 0, 0)), ([twin(own)], (0, 0, 1))])
    side, up, down, mine, acc = lax.optimization_barrier((side, up, down, mine, acc))
    mine = exchange(mine)
    across_up = route(up, 1, 0, 0)
    over = route(up, 0, 1, 0)
    across_down = route(side, 0, -1, 0)
    acc = gathered(
        acc,
        [
            ([side], (1, 0, 0)),
            ([up], (0, -1, 0)),
            ([down], (0, 1, 0)),
            ([twin(side)], (1, 0, 1)),
            ([twin(up)], (0, -1, 1)),
            ([twin(down)], (0, 1, 1)),
        ],
    )
    across_up, over, across_down, acc = lax.optimization_barrier(
        (across_up, over, across_down, acc)
    )
    last = [route(across_up[:half], 0, 1, 0), route(across_down[half:], 0, -1, 0)]
    acc = gathered(
        acc,
        [
            ([over], (0, 2, 0)),
            ([across_up], (1, -1, 0)),
            ([across_down], (1, 1, 0)),
            ([twin(over)], (0, 2, 1)),
            ([twin(across_up)], (1, -1, 1)),
            ([twin(across_down)], (1, 1, 1)),
        ],
    )
    last[0], last[1], acc = lax.optimization_barrier((last[0], last[1], acc))
    placed = gathered(
        acc,
        [(last, (1, 2, 0)), ([twin(b) for b in last], (1, 2, 1))],
        last=True,
        out=placing,
    )
    pre = across(mine, w_self) + across(exchange(placed), w_neigh)
    filled = jnp.sum((part_map[0] == column).astype(jnp.int32)) * TILE
    row = lax.broadcasted_iota(jnp.int32, (capacity * TILE, 1), 0)
    hidden = jnp.where(row < filled, jnp.maximum(pre + bias[None, :], 0.0), 0.0)
    return hidden.astype(jnp.bfloat16)[None, None]


def solution(mesh):
    placed = (
        P("blk", "bal"),
        P("blk", None, None, None, None),
        P("blk", None, None),
        P("blk", None, None),
        P("blk", None),
        P(),
        P(),
        P(),
        P("blk", None),
    )
    return jax.shard_map(
        on_device,
        mesh=mesh,
        in_specs=placed,
        out_specs=P("blk", "bal", None, None),
        check_vma=False,
    )
```

```python
import functools

import jax
import jax.numpy as jnp
from jax import lax
from jax.experimental import pallas as pl
from jax.experimental.pallas import tpu as pltpu
from jax.sharding import PartitionSpec as P

TILE = 128
ONES = 16
UNROLL = 8
AHEAD = 3
SPLIT = 8


def spot(position):
    return position // 8, (position // 2) % 4, position % 2


def route(block, dx, dy, dc):
    pairs = []
    for source in range(16):
        x, y, c = spot(source)
        pairs.append((source, ((x + dx) % 2) * 8 + ((y + dy) % 4) * 2 + (c + dc) % 2))
    return lax.ppermute(block, "blk", pairs)


def absorb(acc_ref, halves, source, table, v_ref):
    slots = v_ref.shape[0]
    live = table[source, 2 * slots]
    dummy = acc_ref.shape[0] - 1

    def step(group, carry):
        found = []
        for u in range(UNROLL):
            slot = group * UNROLL + u
            start = pl.multiple_of(table[source, slots + slot] * TILE, TILE)
            parts = [ref[:, pl.ds(start, TILE)] for ref in halves]
            parts.append(jnp.ones((ONES, TILE), jnp.bfloat16))
            left = jnp.concatenate(parts, axis=0)
            prod = lax.dot_general(
                left, v_ref[slot], (((1,), (1,)), ((), ())), preferred_element_type=jnp.float32
            )
            found.append((jnp.where(slot < live, table[source, slot], dummy), prod))
        for target, prod in found:
            acc_ref[target] += prod
        return carry

    lax.fori_loop(0, (live + UNROLL - 1) // UNROLL, step, 0)


def seat(here, dx, dy, dc):
    x, y, c = here // 8, (here // 2) % 4, here % 2
    return ((x + dx) % 2) * 8 + ((y + dy) % 4) * 2 + (c + dc) % 2


def begin(copy):
    copy.start()


def finish(copy):
    copy.wait()


def act_on(act, make, i, q):
    act(make(i, q))


def gather_kernel(layout, offsets, height, first, last, table, *refs):
    refs = list(refs)
    v_hbm = refs.pop(0)
    n_blocks = sum(layout)
    n = len(layout)
    blocks = [refs.pop(0) for i in range(n_blocks)]
    acc_in = None if first else refs.pop(0)
    out_ref = refs.pop(0)
    v_ref, v_sem, b_sem = refs.pop(0), refs.pop(0), refs.pop(0)
    staged = [refs.pop(0) for i in range(n_blocks)]
    acc_ref, a_sem, o_sem = refs.pop(0), refs.pop(0), refs.pop(0)
    made_ref, used = refs if last else (acc_ref, None)
    slots = v_ref.shape[1]
    here = table[0, 2 * slots + 1]
    places = [seat(here, *offsets[i]) for i in range(n)]
    tiles_per = acc_ref.shape[0] - 1
    span = tiles_per // SPLIT
    loads = []
    if not first:
        for k in range(SPLIT):
            part = pl.ds(k * span, span)
            loads.append(pltpu.make_async_copy(acc_in.at[part], acc_ref.at[part], a_sem.at[k]))
    for copy in loads:
        copy.start()
    parts = v_ref.shape[1] // UNROLL
    begins = [sum(layout[:i]) for i in range(n)]

    def values_copy(i, q):
        part = pl.ds(q * UNROLL, UNROLL)
        return pltpu.make_async_copy(
            v_hbm.at[places[i], part], v_ref.at[i, part], v_sem.at[i * parts + q]
        )

    def each(i, act):
        for j in range(begins[i], begins[i] + layout[i]):
            act(pltpu.make_async_copy(blocks[j], staged[j], b_sem.at[j]))
        for q in range(parts):
            pl.when(table[places[i], 2 * slots] > q * UNROLL)(functools.partial(act_on, act, values_copy, i, q))

    for i in range(min(AHEAD, n)):
        each(i, begin)
    if first:
        acc_ref[...] = jnp.zeros_like(acc_ref)
    if last:
        made_ref[...] = jnp.zeros_like(made_ref)
    for copy in loads:
        copy.wait()
    for i, width in enumerate(layout):
        if i + AHEAD < n:
            each(i + AHEAD, begin)
        each(i, finish)
        absorb(
            acc_ref, staged[begins[i] : begins[i] + width], places[i], table, v_ref.at[i]
        )
    if last:

        def tile_of(t):
            inverse = 1.0 / (1.0 + acc_ref[t, height : height + 1, :])
            return (acc_ref[t, 0:height, :] * inverse).astype(jnp.bfloat16)

        place_into(made_ref, table, used, tiles_per, tile_of)
    step = out_ref.shape[0] // SPLIT
    stores = [
        pltpu.make_async_copy(
            made_ref.at[pl.ds(k * step, step)], out_ref.at[pl.ds(k * step, step)], o_sem.at[k]
        )
        for k in range(SPLIT)
    ]
    for copy in stores:
        copy.start()
    for copy in stores:
        copy.wait()


def accumulate(acc, groups, offsets, table, values, tiles_per, last=False, out=None):
    layout = tuple(len(g) for g in groups)
    blocks = [b for g in groups for b in g]
    height = sum(b.shape[0] for b in groups[0])
    first = acc is None
    smem = pl.BlockSpec(memory_space=pltpu.SMEM)
    anywhere = pl.BlockSpec(memory_space=pl.ANY)
    operands = [table]
    specs = [smem] + [anywhere] * (1 + len(blocks))
    operands += [values] + blocks
    if not first:
        operands.append(acc)
        specs.append(anywhere)
    shape = (tiles_per, height + ONES, TILE)
    scratch = [
        pltpu.VMEM((len(groups),) + values.shape[1:], values.dtype),
        pltpu.SemaphoreType.DMA((len(groups) * (values.shape[1] // UNROLL),)),
        pltpu.SemaphoreType.DMA((len(blocks),)),
    ] + [pltpu.VMEM(b.shape, b.dtype) for b in blocks]
    scratch += [
        pltpu.VMEM((tiles_per + 1,) + shape[1:], jnp.float32),
        pltpu.SemaphoreType.DMA((SPLIT,)),
        pltpu.SemaphoreType.DMA((SPLIT,)),
    ]
    if last:
        made = (out[0], height, out[1])
        scratch += [pltpu.VMEM(made, jnp.bfloat16), pltpu.SMEM((out[0],), jnp.int32)]
        result = jax.ShapeDtypeStruct(made, jnp.bfloat16)
    else:
        result = jax.ShapeDtypeStruct(shape, jnp.float32)
    return pl.pallas_call(
        functools.partial(gather_kernel, layout, tuple(offsets), height, first, last),
        in_specs=specs,
        out_specs=anywhere,
        out_shape=result,
        scratch_shapes=scratch,
        cost_estimate=pl.CostEstimate(
            flops=0, transcendentals=0, bytes_accessed=(8 + 3 * len(groups)) * 2**20
        ),
        name="aggregate_last" if last else "aggregate",
    )(*operands)


def cut_kernel(up_ref, down_ref, *refs):
    top_ref, bottom_ref, held, in_sem, out_sem = refs
    rows = held.shape[1]
    half = top_ref.shape[0]
    loads, stores = [], []
    for k in range(held.shape[0]):
        at = k * rows
        source, target = (up_ref, top_ref) if at < half else (down_ref, bottom_ref)
        loads.append(
            pltpu.make_async_copy(source.at[pl.ds(at, rows)], held.at[k], in_sem.at[k])
        )
        stores.append(
            pltpu.make_async_copy(held.at[k], target.at[pl.ds(at % half, rows)], out_sem.at[k])
        )
    for copy in loads:
        copy.start()
    for load, store in zip(loads, stores):
        load.wait()
        store.start()
    for copy in stores:
        copy.wait()


def cut(up, down):
    anywhere = pl.BlockSpec(memory_space=pl.ANY)
    piece = jax.ShapeDtypeStruct((up.shape[0] // 2, up.shape[1]), up.dtype)
    return pl.pallas_call(
        cut_kernel,
        in_specs=[anywhere] * 2,
        out_specs=[anywhere] * 2,
        out_shape=[piece] * 2,
        scratch_shapes=[pltpu.VMEM((4, up.shape[0] // 4, up.shape[1]), up.dtype)]
        + [pltpu.SemaphoreType.DMA((4,))] * 2,
        name="cut",
    )(up, down)


def place_into(out_ref, mapping, used, tiles_per, tile_of):
    n_bal = out_ref.shape[0]
    out_ref[...] = jnp.zeros_like(out_ref)
    for d in range(n_bal):
        used[d] = 0

    def step(t, carry):
        d = mapping[mapping.shape[0] - 1, t]
        k = used[d]
        used[d] = k + 1
        out_ref[d, :, pl.ds(pl.multiple_of(k * TILE, TILE), TILE)] = tile_of(t)
        return carry

    lax.fori_loop(0, tiles_per, step, 0, unroll=8)


def place_kernel(mapping, x_ref, out_ref, used):
    tiles_per = x_ref.shape[1] // TILE
    place_into(
        out_ref, mapping, used, tiles_per,
        lambda t: x_ref[:, pl.ds(pl.multiple_of(t * TILE, TILE), TILE)],
    )


def place_features(block, mapping, n_bal, capacity):
    return pl.pallas_call(
        place_kernel,
        in_specs=[pl.BlockSpec(memory_space=pltpu.SMEM), pl.BlockSpec(memory_space=pltpu.VMEM)],
        out_specs=pl.BlockSpec(memory_space=pltpu.VMEM),
        out_shape=jax.ShapeDtypeStruct((n_bal, block.shape[0], capacity * TILE), block.dtype),
        scratch_shapes=[pltpu.SMEM((n_bal,), jnp.int32)],
        cost_estimate=pl.CostEstimate(flops=0, transcendentals=0, bytes_accessed=8 * 2**20),
        name="place_features",
    )(mapping, block)


def fit(table):
    return jnp.pad(table, ((0, 0), (0, TILE - table.shape[1])))


def exchange(placed):
    got = lax.all_to_all(placed, "bal", split_axis=0, concat_axis=0, tiled=True)
    return got.reshape(got.shape[0] * got.shape[1], got.shape[2])


def across(left, right):
    return lax.dot_general(
        left, right, (((0,), (0,)), ((), ())), preferred_element_type=jnp.float32
    )


def on_device(
    features, tile_values, tile_rows, tile_cols, tile_counts, w_self, w_neigh, bias, part_map
):
    n_blk = lax.axis_size("blk")
    n_bal = lax.axis_size("bal")
    here = lax.axis_index("blk")
    column = lax.axis_index("bal")
    tiles_per = part_map.shape[1]
    capacity = 2 * tiles_per // n_bal
    width = features.shape[1]
    values = tile_values[0]
    table = jnp.concatenate(
        [tile_rows[0], tile_cols[0], tile_counts[0][:, None], jnp.full((n_blk, 1), here)], axis=1
    ).astype(jnp.int32)
    table = jnp.concatenate([fit(table), fit(part_map.astype(jnp.int32))], axis=0)
    own = features.T
    placing = (n_bal, capacity * TILE)

    def gathered(acc, pieces, **extra):
        groups = [list(blocks) for blocks, offset in pieces]
        offsets = [offset for blocks, offset in pieces]
        return accumulate(acc, groups, offsets, table, values, tiles_per, **extra)

    def twin(block):
        return route(block, 0, 0, 1)

    side = route(own, 1, 0, 0)
    up = route(own, 0, 1, 0)
    down = route(own, 0, -1, 0)
    mine = place_features(own, table, n_bal, capacity)
    acc = gathered(None, [([own], (0, 0, 0)), ([twin(own)], (0, 0, 1))])
    side, up, down, mine, acc = lax.optimization_barrier((side, up, down, mine, acc))
    mine = exchange(mine)
    across_up = route(up, 1, 0, 0)
    over = route(up, 0, 1, 0)
    across_down = route(side, 0, -1, 0)
    acc = gathered(
        acc,
        [
            ([side], (1, 0, 0)),
            ([up], (0, -1, 0)),
            ([down], (0, 1, 0)),
            ([twin(side)], (1, 0, 1)),
            ([twin(up)], (0, -1, 1)),
            ([twin(down)], (0, 1, 1)),
        ],
    )
    across_up, over, across_down, acc = lax.optimization_barrier(
        (across_up, over, across_down, acc)
    )
    top, bottom = cut(across_up, across_down)
    last = [route(top, 0, 1, 0), route(bottom, 0, -1, 0)]
    acc = gathered(
        acc,
        [
            ([over], (0, 2, 0)),
            ([across_up], (1, -1, 0)),
            ([across_down], (1, 1, 0)),
            ([twin(over)], (0, 2, 1)),
            ([twin(across_up)], (1, -1, 1)),
            ([twin(across_down)], (1, 1, 1)),
        ],
    )
    last[0], last[1], acc = lax.optimization_barrier((last[0], last[1], acc))
    placed = gathered(
        acc,
        [(last, (1, 2, 0)), ([twin(b) for b in last], (1, 2, 1))],
        last=True,
        out=placing,
    )
    means, mine = lax.optimization_barrier((exchange(placed), mine))
    pre = across(means, w_neigh) + across(mine, w_self)
    filled = jnp.sum((part_map[0] == column).astype(jnp.int32)) * TILE
    row = lax.broadcasted_iota(jnp.int32, (capacity * TILE, 1), 0)
    hidden = jnp.where(row < filled, jnp.maximum(pre + bias[None, :], 0.0), 0.0)
    return hidden.astype(jnp.bfloat16)[None, None]


def solution(mesh):
    placed = (
        P("blk", "bal"),
        P("blk", None, None, None, None),
        P("blk", None, None),
        P("blk", None, None),
        P("blk", None),
        P(),
        P(),
        P(),
        P("blk", None),
    )
    return jax.shard_map(
        on_device,
        mesh=mesh,
        in_specs=placed,
        out_specs=P("blk", "bal", None, None),
        check_vma=False,
    )
```

```python
import functools

import jax
import jax.numpy as jnp
from jax import lax
from jax.experimental import pallas as pl
from jax.experimental.pallas import tpu as pltpu
from jax.sharding import PartitionSpec as P

TILE = 128
ONES = 16
UNROLL = 8
AHEAD = 3
SPLIT = 8


def spot(position):
    return position // 8, (position // 2) % 4, position % 2


def route(block, dx, dy, dc):
    pairs = []
    for source in range(16):
        x, y, c = spot(source)
        pairs.append((source, ((x + dx) % 2) * 8 + ((y + dy) % 4) * 2 + (c + dc) % 2))
    return lax.ppermute(block, "blk", pairs)


def absorb(acc_ref, halves, source, table, v_ref):
    slots = v_ref.shape[0]
    live = table[source, 2 * slots]
    dummy = acc_ref.shape[0] - 1

    def step(group, carry):
        found = []
        for u in range(UNROLL):
            slot = group * UNROLL + u
            start = pl.multiple_of(table[source, slots + slot] * TILE, TILE)
            parts = [ref[:, pl.ds(start, TILE)] for ref in halves]
            parts.append(jnp.ones((ONES, TILE), jnp.bfloat16))
            left = jnp.concatenate(parts, axis=0)
            prod = lax.dot_general(
                left, v_ref[slot], (((1,), (1,)), ((), ())), preferred_element_type=jnp.float32
            )
            found.append((jnp.where(slot < live, table[source, slot], dummy), prod))
        for target, prod in found:
            acc_ref[target] += prod
        return carry

    lax.fori_loop(0, (live + UNROLL - 1) // UNROLL, step, 0)


def seat(here, dx, dy, dc):
    x, y, c = here // 8, (here // 2) % 4, here % 2
    return ((x + dx) % 2) * 8 + ((y + dy) % 4) * 2 + (c + dc) % 2


def begin(copy):
    copy.start()


def finish(copy):
    copy.wait()


def act_on(act, make, i, q):
    act(make(i, q))


def gather_kernel(layout, offsets, height, first, last, table, *refs):
    refs = list(refs)
    v_hbm = refs.pop(0)
    n_blocks = sum(layout)
    n = len(layout)
    blocks = [refs.pop(0) for i in range(n_blocks)]
    acc_in = None if first else refs.pop(0)
    out_ref = refs.pop(0)
    v_ref, v_sem, b_sem = refs.pop(0), refs.pop(0), refs.pop(0)
    staged = [refs.pop(0) for i in range(n_blocks)]
    acc_ref, a_sem, o_sem = refs.pop(0), refs.pop(0), refs.pop(0)
    made_ref, used = refs if last else (acc_ref, None)
    slots = v_ref.shape[1]
    here = table[0, 2 * slots + 1]
    places = [seat(here, *offsets[i]) for i in range(n)]
    tiles_per = acc_ref.shape[0] - 1
    span = tiles_per // SPLIT
    loads = []
    if not first:
        for k in range(SPLIT):
            part = pl.ds(k * span, span)
            loads.append(pltpu.make_async_copy(acc_in.at[part], acc_ref.at[part], a_sem.at[k]))
    for copy in loads:
        copy.start()
    parts = v_ref.shape[1] // UNROLL
    begins = [sum(layout[:i]) for i in range(n)]

    def values_copy(i, q):
        part = pl.ds(q * UNROLL, UNROLL)
        return pltpu.make_async_copy(
            v_hbm.at[places[i], part], v_ref.at[i, part], v_sem.at[i * parts + q]
        )

    def each(i, act):
        for j in range(begins[i], begins[i] + layout[i]):
            act(pltpu.make_async_copy(blocks[j], staged[j], b_sem.at[j]))
        for q in range(parts):
            pl.when(table[places[i], 2 * slots] > q * UNROLL)(functools.partial(act_on, act, values_copy, i, q))

    for i in range(min(AHEAD, n)):
        each(i, begin)
    if first:
        acc_ref[...] = jnp.zeros_like(acc_ref)
    if last:
        made_ref[...] = jnp.zeros_like(made_ref)
    for copy in loads:
        copy.wait()
    for i, width in enumerate(layout):
        if i + AHEAD < n:
            each(i + AHEAD, begin)
        each(i, finish)
        absorb(
            acc_ref, staged[begins[i] : begins[i] + width], places[i], table, v_ref.at[i]
        )
    if last:

        def tile_of(t):
            inverse = 1.0 / (1.0 + acc_ref[t, height : height + 1, :])
            return (acc_ref[t, 0:height, :] * inverse).astype(jnp.bfloat16)

        place_into(made_ref, table, used, tiles_per, tile_of)
    step = out_ref.shape[0] // SPLIT
    stores = [
        pltpu.make_async_copy(
            made_ref.at[pl.ds(k * step, step)], out_ref.at[pl.ds(k * step, step)], o_sem.at[k]
        )
        for k in range(SPLIT)
    ]
    for copy in stores:
        copy.start()
    for copy in stores:
        copy.wait()


def accumulate(acc, groups, offsets, table, values, tiles_per, last=False, out=None):
    layout = tuple(len(g) for g in groups)
    blocks = [b for g in groups for b in g]
    height = sum(b.shape[0] for b in groups[0])
    first = acc is None
    smem = pl.BlockSpec(memory_space=pltpu.SMEM)
    anywhere = pl.BlockSpec(memory_space=pl.ANY)
    operands = [table]
    held = [last and offset[2] == 1 for g, offset in zip(groups, offsets) for b in g]
    near = pl.BlockSpec(memory_space=pltpu.VMEM)
    specs = [smem, anywhere] + [near if h else anywhere for h in held]
    blocks = [
        pltpu.with_memory_space_constraint(b, pltpu.VMEM) if h else b for b, h in zip(blocks, held)
    ]
    operands += [values] + blocks
    if not first:
        operands.append(acc)
        specs.append(anywhere)
    shape = (tiles_per, height + ONES, TILE)
    scratch = [
        pltpu.VMEM((len(groups),) + values.shape[1:], values.dtype),
        pltpu.SemaphoreType.DMA((len(groups) * (values.shape[1] // UNROLL),)),
        pltpu.SemaphoreType.DMA((len(blocks),)),
    ] + [pltpu.VMEM(b.shape, b.dtype) for b in blocks]
    scratch += [
        pltpu.VMEM((tiles_per + 1,) + shape[1:], jnp.float32),
        pltpu.SemaphoreType.DMA((SPLIT,)),
        pltpu.SemaphoreType.DMA((SPLIT,)),
    ]
    if last:
        made = (out[0], height, out[1])
        scratch += [pltpu.VMEM(made, jnp.bfloat16), pltpu.SMEM((out[0],), jnp.int32)]
        result = jax.ShapeDtypeStruct(made, jnp.bfloat16)
    else:
        result = jax.ShapeDtypeStruct(shape, jnp.float32)
    return pl.pallas_call(
        functools.partial(gather_kernel, layout, tuple(offsets), height, first, last),
        in_specs=specs,
        out_specs=anywhere,
        out_shape=result,
        scratch_shapes=scratch,
        cost_estimate=pl.CostEstimate(
            flops=0, transcendentals=0, bytes_accessed=(8 + 3 * len(groups)) * 2**20
        ),
        name="aggregate_last" if last else "aggregate",
    )(*operands)


def cut_kernel(up_ref, down_ref, *refs):
    top_ref, bottom_ref, held, in_sem, out_sem = refs
    rows = held.shape[1]
    half = top_ref.shape[0]
    loads, stores = [], []
    for k in range(held.shape[0]):
        at = k * rows
        source, target = (up_ref, top_ref) if at < half else (down_ref, bottom_ref)
        loads.append(
            pltpu.make_async_copy(source.at[pl.ds(at, rows)], held.at[k], in_sem.at[k])
        )
        stores.append(
            pltpu.make_async_copy(held.at[k], target.at[pl.ds(at % half, rows)], out_sem.at[k])
        )
    for copy in loads:
        copy.start()
    for load, store in zip(loads, stores):
        load.wait()
        store.start()
    for copy in stores:
        copy.wait()


def cut(up, down):
    anywhere = pl.BlockSpec(memory_space=pl.ANY)
    piece = jax.ShapeDtypeStruct((up.shape[0] // 2, up.shape[1]), up.dtype)
    return pl.pallas_call(
        cut_kernel,
        in_specs=[anywhere] * 2,
        out_specs=[anywhere] * 2,
        out_shape=[piece] * 2,
        scratch_shapes=[pltpu.VMEM((4, up.shape[0] // 4, up.shape[1]), up.dtype)]
        + [pltpu.SemaphoreType.DMA((4,))] * 2,
        name="cut",
    )(up, down)


def place_into(out_ref, mapping, used, tiles_per, tile_of):
    n_bal = out_ref.shape[0]
    out_ref[...] = jnp.zeros_like(out_ref)
    for d in range(n_bal):
        used[d] = 0

    def step(t, carry):
        d = mapping[mapping.shape[0] - 1, t]
        k = used[d]
        used[d] = k + 1
        out_ref[d, :, pl.ds(pl.multiple_of(k * TILE, TILE), TILE)] = tile_of(t)
        return carry

    lax.fori_loop(0, tiles_per, step, 0, unroll=8)


def place_kernel(mapping, x_ref, out_ref, used):
    tiles_per = x_ref.shape[1] // TILE
    place_into(
        out_ref, mapping, used, tiles_per,
        lambda t: x_ref[:, pl.ds(pl.multiple_of(t * TILE, TILE), TILE)],
    )


def place_features(block, mapping, n_bal, capacity):
    return pl.pallas_call(
        place_kernel,
        in_specs=[pl.BlockSpec(memory_space=pltpu.SMEM), pl.BlockSpec(memory_space=pltpu.VMEM)],
        out_specs=pl.BlockSpec(memory_space=pltpu.VMEM),
        out_shape=jax.ShapeDtypeStruct((n_bal, block.shape[0], capacity * TILE), block.dtype),
        scratch_shapes=[pltpu.SMEM((n_bal,), jnp.int32)],
        cost_estimate=pl.CostEstimate(flops=0, transcendentals=0, bytes_accessed=8 * 2**20),
        name="place_features",
    )(mapping, block)


def fit(table):
    return jnp.pad(table, ((0, 0), (0, TILE - table.shape[1])))


def exchange(placed):
    got = lax.all_to_all(placed, "bal", split_axis=0, concat_axis=0, tiled=True)
    return got.reshape(got.shape[0] * got.shape[1], got.shape[2])


def across(left, right):
    return lax.dot_general(
        left, right, (((0,), (0,)), ((), ())), preferred_element_type=jnp.float32
    )


def on_device(
    features, tile_values, tile_rows, tile_cols, tile_counts, w_self, w_neigh, bias, part_map
):
    n_blk = lax.axis_size("blk")
    n_bal = lax.axis_size("bal")
    here = lax.axis_index("blk")
    column = lax.axis_index("bal")
    tiles_per = part_map.shape[1]
    capacity = 2 * tiles_per // n_bal
    width = features.shape[1]
    values = tile_values[0]
    table = jnp.concatenate(
        [tile_rows[0], tile_cols[0], tile_counts[0][:, None], jnp.full((n_blk, 1), here)], axis=1
    ).astype(jnp.int32)
    table = jnp.concatenate([fit(table), fit(part_map.astype(jnp.int32))], axis=0)
    own = features.T
    placing = (n_bal, capacity * TILE)

    def gathered(acc, pieces, **extra):
        groups = [list(blocks) for blocks, offset in pieces]
        offsets = [offset for blocks, offset in pieces]
        return accumulate(acc, groups, offsets, table, values, tiles_per, **extra)

    def twin(block):
        return route(block, 0, 0, 1)

    side = route(own, 1, 0, 0)
    up = route(own, 0, 1, 0)
    down = route(own, 0, -1, 0)
    mine = place_features(own, table, n_bal, capacity)
    acc = gathered(None, [([own], (0, 0, 0)), ([twin(own)], (0, 0, 1))])
    side, up, down, mine, acc = lax.optimization_barrier((side, up, down, mine, acc))
    mine = exchange(mine)
    across_up = route(up, 1, 0, 0)
    over = route(up, 0, 1, 0)
    across_down = route(side, 0, -1, 0)
    acc = gathered(
        acc,
        [
            ([side], (1, 0, 0)),
            ([up], (0, -1, 0)),
            ([down], (0, 1, 0)),
            ([twin(side)], (1, 0, 1)),
            ([twin(up)], (0, -1, 1)),
            ([twin(down)], (0, 1, 1)),
        ],
    )
    across_up, over, across_down, acc = lax.optimization_barrier(
        (across_up, over, across_down, acc)
    )
    top, bottom = cut(across_up, across_down)
    last = [route(top, 0, 1, 0), route(bottom, 0, -1, 0)]
    acc = gathered(
        acc,
        [
            ([over], (0, 2, 0)),
            ([across_up], (1, -1, 0)),
            ([across_down], (1, 1, 0)),
            ([twin(over)], (0, 2, 1)),
            ([twin(across_up)], (1, -1, 1)),
            ([twin(across_down)], (1, 1, 1)),
        ],
    )
    last[0], last[1], acc = lax.optimization_barrier((last[0], last[1], acc))
    placed = gathered(
        acc,
        [(last, (1, 2, 0)), ([twin(b) for b in last], (1, 2, 1))],
        last=True,
        out=placing,
    )
    pre = across(mine, w_self) + across(exchange(placed), w_neigh)
    filled = jnp.sum((part_map[0] == column).astype(jnp.int32)) * TILE
    row = lax.broadcasted_iota(jnp.int32, (capacity * TILE, 1), 0)
    hidden = jnp.where(row < filled, jnp.maximum(pre + bias[None, :], 0.0), 0.0)
    return hidden.astype(jnp.bfloat16)[None, None]


def solution(mesh):
    placed = (
        P("blk", "bal"),
        P("blk", None, None, None, None),
        P("blk", None, None),
        P("blk", None, None),
        P("blk", None),
        P(),
        P(),
        P(),
        P("blk", None),
    )
    return jax.shard_map(
        on_device,
        mesh=mesh,
        in_specs=placed,
        out_specs=P("blk", "bal", None, None),
        check_vma=False,
    )
```

```python
import functools

import jax
import jax.numpy as jnp
from jax import lax
from jax.experimental import pallas as pl
from jax.experimental.pallas import tpu as pltpu
from jax.sharding import PartitionSpec as P

TILE = 128
ONES = 16
UNROLL = 8
AHEAD = 3
SPLIT = 8


def spot(position):
    return position // 8, (position // 2) % 4, position % 2


def route(block, dx, dy, dc):
    pairs = []
    for source in range(16):
        x, y, c = spot(source)
        pairs.append((source, ((x + dx) % 2) * 8 + ((y + dy) % 4) * 2 + (c + dc) % 2))
    return lax.ppermute(block, "blk", pairs)


def absorb(acc_ref, halves, source, table, v_ref):
    slots = v_ref.shape[0]
    live = table[source, 2 * slots]
    dummy = acc_ref.shape[0] - 1

    def step(group, carry):
        found = []
        for u in range(UNROLL):
            slot = group * UNROLL + u
            start = pl.multiple_of(table[source, slots + slot] * TILE, TILE)
            parts = [ref[:, pl.ds(start, TILE)] for ref in halves]
            parts.append(jnp.ones((ONES, TILE), jnp.bfloat16))
            left = jnp.concatenate(parts, axis=0)
            prod = lax.dot_general(
                left, v_ref[slot], (((1,), (1,)), ((), ())), preferred_element_type=jnp.float32
            )
            found.append((jnp.where(slot < live, table[source, slot], dummy), prod))
        for target, prod in found:
            acc_ref[target] += prod
        return carry

    lax.fori_loop(0, (live + UNROLL - 1) // UNROLL, step, 0)


def seat(here, dx, dy, dc):
    x, y, c = here // 8, (here // 2) % 4, here % 2
    return ((x + dx) % 2) * 8 + ((y + dy) % 4) * 2 + (c + dc) % 2


def begin(copy):
    copy.start()


def finish(copy):
    copy.wait()


def act_on(act, make, i, q):
    act(make(i, q))


def gather_kernel(layout, offsets, height, first, last, table, *refs):
    refs = list(refs)
    v_hbm = refs.pop(0)
    n_blocks = sum(layout)
    n = len(layout)
    blocks = [refs.pop(0) for i in range(n_blocks)]
    acc_in = None if first else refs.pop(0)
    out_ref = refs.pop(0)
    v_ref, v_sem, b_sem = refs.pop(0), refs.pop(0), refs.pop(0)
    staged = [refs.pop(0) for i in range(n_blocks)]
    acc_ref, a_sem, o_sem = refs.pop(0), refs.pop(0), refs.pop(0)
    made_ref, used = refs if last else (acc_ref, None)
    slots = v_ref.shape[1]
    here = table[0, 2 * slots + 1]
    places = [seat(here, *offsets[i]) for i in range(n)]
    tiles_per = acc_ref.shape[0] - 1
    span = tiles_per // SPLIT
    loads = []
    if not first:
        for k in range(SPLIT):
            part = pl.ds(k * span, span)
            loads.append(pltpu.make_async_copy(acc_in.at[part], acc_ref.at[part], a_sem.at[k]))
    for copy in loads:
        copy.start()
    parts = v_ref.shape[1] // UNROLL
    begins = [sum(layout[:i]) for i in range(n)]

    def values_copy(i, q):
        part = pl.ds(q * UNROLL, UNROLL)
        return pltpu.make_async_copy(
            v_hbm.at[places[i], part], v_ref.at[i, part], v_sem.at[i * parts + q]
        )

    def each(i, act):
        for j in range(begins[i], begins[i] + layout[i]):
            act(pltpu.make_async_copy(blocks[j], staged[j], b_sem.at[j]))
        for q in range(parts):
            pl.when(table[places[i], 2 * slots] > q * UNROLL)(functools.partial(act_on, act, values_copy, i, q))

    for i in range(min(AHEAD, n)):
        each(i, begin)
    if first:
        acc_ref[...] = jnp.zeros_like(acc_ref)
    if last:
        made_ref[...] = jnp.zeros_like(made_ref)
    for copy in loads:
        copy.wait()
    for i, width in enumerate(layout):
        if i + AHEAD < n:
            each(i + AHEAD, begin)
        each(i, finish)
        absorb(
            acc_ref, staged[begins[i] : begins[i] + width], places[i], table, v_ref.at[i]
        )
    if last:

        def tile_of(t):
            inverse = 1.0 / (1.0 + acc_ref[t, height : height + 1, :])
            return (acc_ref[t, 0:height, :] * inverse).astype(jnp.bfloat16)

        place_into(made_ref, table, used, tiles_per, tile_of)
    step = out_ref.shape[0] // SPLIT
    stores = [
        pltpu.make_async_copy(
            made_ref.at[pl.ds(k * step, step)], out_ref.at[pl.ds(k * step, step)], o_sem.at[k]
        )
        for k in range(SPLIT)
    ]
    for copy in stores:
        copy.start()
    for copy in stores:
        copy.wait()


def accumulate(acc, groups, offsets, table, values, tiles_per, last=False, out=None):
    layout = tuple(len(g) for g in groups)
    blocks = [b for g in groups for b in g]
    height = sum(b.shape[0] for b in groups[0])
    first = acc is None
    smem = pl.BlockSpec(memory_space=pltpu.SMEM)
    anywhere = pl.BlockSpec(memory_space=pl.ANY)
    operands = [table]
    held = [last and offset[2] == 1 for g, offset in zip(groups, offsets) for b in g]
    near = pl.BlockSpec(memory_space=pltpu.VMEM)
    specs = [smem, anywhere] + [near if h else anywhere for h in held]
    blocks = [
        pltpu.with_memory_space_constraint(b, pltpu.VMEM) if h else b for b, h in zip(blocks, held)
    ]
    operands += [values] + blocks
    if not first:
        operands.append(acc)
        specs.append(anywhere)
    shape = (tiles_per, height + ONES, TILE)
    scratch = [
        pltpu.VMEM((len(groups),) + values.shape[1:], values.dtype),
        pltpu.SemaphoreType.DMA((len(groups) * (values.shape[1] // UNROLL),)),
        pltpu.SemaphoreType.DMA((len(blocks),)),
    ] + [pltpu.VMEM(b.shape, b.dtype) for b in blocks]
    scratch += [
        pltpu.VMEM((tiles_per + 1,) + shape[1:], jnp.float32),
        pltpu.SemaphoreType.DMA((SPLIT,)),
        pltpu.SemaphoreType.DMA((SPLIT,)),
    ]
    if last:
        made = (out[0], height, out[1])
        scratch += [pltpu.VMEM(made, jnp.bfloat16), pltpu.SMEM((out[0],), jnp.int32)]
        result = jax.ShapeDtypeStruct(made, jnp.bfloat16)
    else:
        result = jax.ShapeDtypeStruct(shape, jnp.float32)
    return pl.pallas_call(
        functools.partial(gather_kernel, layout, tuple(offsets), height, first, last),
        in_specs=specs,
        out_specs=anywhere,
        out_shape=result,
        scratch_shapes=scratch,
        cost_estimate=pl.CostEstimate(
            flops=0, transcendentals=0, bytes_accessed=(8 + 3 * len(groups)) * 2**20
        ),
        name="aggregate_last" if last else "aggregate",
    )(*operands)


def cut_kernel(up_ref, down_ref, top_ref, bottom_ref, sems):
    half = top_ref.shape[0]
    rows = half // 2
    copies = []
    for k in range(4):
        at = k * rows
        source, target = (up_ref, top_ref) if at < half else (down_ref, bottom_ref)
        copies.append(
            pltpu.make_async_copy(
                source.at[pl.ds(at, rows)], target.at[pl.ds(at % half, rows)], sems.at[k]
            )
        )
    for copy in copies:
        copy.start()
    for copy in copies:
        copy.wait()


def cut(up, down):
    piece = jax.ShapeDtypeStruct((up.shape[0] // 2, up.shape[1]), up.dtype)
    return pl.pallas_call(
        cut_kernel,
        in_specs=[pl.BlockSpec(memory_space=pltpu.VMEM)] * 2,
        out_specs=[pl.BlockSpec(memory_space=pl.ANY)] * 2,
        out_shape=[piece] * 2,
        scratch_shapes=[pltpu.SemaphoreType.DMA((4,))],
        name="cut",
    )(*[pltpu.with_memory_space_constraint(b, pltpu.VMEM) for b in (up, down)])


def place_into(out_ref, mapping, used, tiles_per, tile_of):
    n_bal = out_ref.shape[0]
    out_ref[...] = jnp.zeros_like(out_ref)
    for d in range(n_bal):
        used[d] = 0

    def step(t, carry):
        d = mapping[mapping.shape[0] - 1, t]
        k = used[d]
        used[d] = k + 1
        out_ref[d, :, pl.ds(pl.multiple_of(k * TILE, TILE), TILE)] = tile_of(t)
        return carry

    lax.fori_loop(0, tiles_per, step, 0, unroll=8)


def place_kernel(mapping, x_ref, out_ref, used):
    tiles_per = x_ref.shape[1] // TILE
    place_into(
        out_ref, mapping, used, tiles_per,
        lambda t: x_ref[:, pl.ds(pl.multiple_of(t * TILE, TILE), TILE)],
    )


def place_features(block, mapping, n_bal, capacity):
    return pl.pallas_call(
        place_kernel,
        in_specs=[pl.BlockSpec(memory_space=pltpu.SMEM), pl.BlockSpec(memory_space=pltpu.VMEM)],
        out_specs=pl.BlockSpec(memory_space=pltpu.VMEM),
        out_shape=jax.ShapeDtypeStruct((n_bal, block.shape[0], capacity * TILE), block.dtype),
        scratch_shapes=[pltpu.SMEM((n_bal,), jnp.int32)],
        cost_estimate=pl.CostEstimate(flops=0, transcendentals=0, bytes_accessed=8 * 2**20),
        name="place_features",
    )(mapping, block)


def fit(table):
    return jnp.pad(table, ((0, 0), (0, TILE - table.shape[1])))


def exchange(placed):
    got = lax.all_to_all(placed, "bal", split_axis=0, concat_axis=0, tiled=True)
    return got.reshape(got.shape[0] * got.shape[1], got.shape[2])


def across(left, right):
    return lax.dot_general(
        left, right, (((0,), (0,)), ((), ())), preferred_element_type=jnp.float32
    )


def on_device(
    features, tile_values, tile_rows, tile_cols, tile_counts, w_self, w_neigh, bias, part_map
):
    n_blk = lax.axis_size("blk")
    n_bal = lax.axis_size("bal")
    here = lax.axis_index("blk")
    column = lax.axis_index("bal")
    tiles_per = part_map.shape[1]
    capacity = 2 * tiles_per // n_bal
    width = features.shape[1]
    values = tile_values[0]
    table = jnp.concatenate(
        [tile_rows[0], tile_cols[0], tile_counts[0][:, None], jnp.full((n_blk, 1), here)], axis=1
    ).astype(jnp.int32)
    table = jnp.concatenate([fit(table), fit(part_map.astype(jnp.int32))], axis=0)
    own = features.T
    placing = (n_bal, capacity * TILE)

    def gathered(acc, pieces, **extra):
        groups = [list(blocks) for blocks, offset in pieces]
        offsets = [offset for blocks, offset in pieces]
        return accumulate(acc, groups, offsets, table, values, tiles_per, **extra)

    def twin(block):
        return route(block, 0, 0, 1)

    side = route(own, 1, 0, 0)
    up = route(own, 0, 1, 0)
    down = route(own, 0, -1, 0)
    mine = place_features(own, table, n_bal, capacity)
    acc = gathered(None, [([own], (0, 0, 0)), ([twin(own)], (0, 0, 1))])
    side, up, down, mine, acc = lax.optimization_barrier((side, up, down, mine, acc))
    mine = exchange(mine)
    across_up = route(up, 1, 0, 0)
    over = route(up, 0, 1, 0)
    across_down = route(side, 0, -1, 0)
    acc = gathered(
        acc,
        [
            ([side], (1, 0, 0)),
            ([up], (0, -1, 0)),
            ([down], (0, 1, 0)),
            ([twin(side)], (1, 0, 1)),
            ([twin(up)], (0, -1, 1)),
            ([twin(down)], (0, 1, 1)),
        ],
    )
    across_up, over, across_down, acc = lax.optimization_barrier(
        (across_up, over, across_down, acc)
    )
    top, bottom = cut(across_up, across_down)
    last = [route(top, 0, 1, 0), route(bottom, 0, -1, 0)]
    acc = gathered(
        acc,
        [
            ([over], (0, 2, 0)),
            ([across_up], (1, -1, 0)),
            ([across_down], (1, 1, 0)),
            ([twin(over)], (0, 2, 1)),
            ([twin(across_up)], (1, -1, 1)),
            ([twin(across_down)], (1, 1, 1)),
        ],
    )
    last[0], last[1], acc = lax.optimization_barrier((last[0], last[1], acc))
    placed = gathered(
        acc,
        [(last, (1, 2, 0)), ([twin(b) for b in last], (1, 2, 1))],
        last=True,
        out=placing,
    )
    pre = across(mine, w_self) + across(exchange(placed), w_neigh)
    filled = jnp.sum((part_map[0] == column).astype(jnp.int32)) * TILE
    row = lax.broadcasted_iota(jnp.int32, (capacity * TILE, 1), 0)
    hidden = jnp.where(row < filled, jnp.maximum(pre + bias[None, :], 0.0), 0.0)
    return hidden.astype(jnp.bfloat16)[None, None]


def solution(mesh):
    placed = (
        P("blk", "bal"),
        P("blk", None, None, None, None),
        P("blk", None, None),
        P("blk", None, None),
        P("blk", None),
        P(),
        P(),
        P(),
        P("blk", None),
    )
    return jax.shard_map(
        on_device,
        mesh=mesh,
        in_specs=placed,
        out_specs=P("blk", "bal", None, None),
        check_vma=False,
    )
```
